256 devices in a mesh: date: 16 (over z, core), tile: 16 (over x, y).
Axes of the slice: x: 4, y: 4, z: 8, core: 2. Of those that a mesh axis runs over, the one named last changes fastest.
Arguments:
- imagery: bfloat16 [10, 64, 65536], P(None, 'date', 'tile'), may hold values from -6 to 6
- owner: int32 [65536, 1], replicated, may hold values from 0 to 15; in each aligned block of 4096 rows (0 to 4095, 4096 to 8191, ...) at most 1024 rows name the same one
- parcel_local: int32 [65536], replicated, may hold values from 0 to 15
- lift_weight: bfloat16 [10, 128], replicated, may hold values from -2 to 2
- depth_weight: float32 [2, 5, 128], replicated, may hold values from -2.5 to 2.5
- point_weight: bfloat16 [2, 128, 128], replicated, may hold values from -0.5 to 0.5
- bn_mean: float32 [2, 128], replicated, may hold values from -0.5 to 0.5
- bn_var: float32 [2, 128], replicated, may hold values from 0.25 to 4
- bn_gain: float32 [2, 128], replicated, may hold values from 0.5 to 2
- bn_shift: float32 [2, 128], replicated, may hold values from -1 to 1
Outputs:
- parcel_means: float32 [16, 256, 128], P('date', 'tile')
The draws below stay inside these ranges and needn't reach their ends.
Inputs may be any that keep to these rules, and one draw needn't show every extreme that they name: `owner`: in each aligned block of 4096 rows (the pixels of one tile), no tile index appears more than 1024 times, and some index appears exactly 1024 times.
All inputs are finite; a program needn't handle non-finite values.
Results may differ from the reference program's by a relative error of at most 0.0008.
Values may be sent and summed in bfloat16 or wider, within the bound.
No kernel may reach another device: no remote copies, remote signals or barrier semaphores. Data moves between devices by JAX's collectives and lax.ppermute only.
A program may use at most 128 MiB of HBM per device.

```python
import math
import jax
import jax.numpy as jnp
import numpy as np
from jax import lax

BANDS = 10
CH = 128
KSIZE = 5
LAYERS = 2
PIX_DEV = 4096
PARC_DEV = 16
DATES = 64
DOUT = 16
CAP = 1024
PIXELS = 65536
PARCELS = 256
N_TILE = 16


def touch_ends(entries, rng, smallest, top_value):
    shape = entries.shape
    spot = [jax.random.randint(jax.random.fold_in(rng, axis), (), 0, shape[axis]) for axis in range(len(shape))]
    entries = entries.at[tuple(spot)].set(smallest)
    longest = shape.index(max(shape))
    spot[longest] = (spot[longest] + 1) % shape[longest]
    return entries.at[tuple(spot)].set(top_value)


def level_of(own_key, shape, shards, smallest, largest):
    def one(dim, shards_of):
        steps = jax.random.uniform(jax.random.fold_in(jax.random.fold_in(own_key, 6), dim), (shards_of,), jnp.float32, smallest / len(shards), largest / len(shards))
        return jnp.repeat(jnp.exp(steps), shape[dim] // shards_of).reshape((-1,) + (1,) * (len(shape) - dim - 1))

    level = one(*shards[0])
    for cut in shards[1:]:
        level = level * one(*cut)
    return level


def rank_bounds(number_of, slope):
    portions = [(1 << 20) // math.isqrt(rank ** slope) + 1 for rank in range(1, number_of + 1)]
    width = 1 + sum(portions) // (1 << 30)
    return np.cumsum(np.array([max(1, weight // width) for weight in portions]))


def skewed_ids(own_key, extent, count, slope):
    table = rank_bounds(count, slope)
    lot = jax.random.randint(jax.random.fold_in(own_key, 1), extent, 0, int(table[count - 1]))
    standing = jnp.searchsorted(jnp.asarray(table, jnp.int32), lot, side="right")
    return jax.random.permutation(jax.random.fold_in(own_key, 2), count)[standing].astype(jnp.int32)


def assign_block(own_key, own, number, rows, count, top, limit, skew):
    ranking = jax.random.permutation(own_key, count)
    heavy_load, usual = portions_of(count, rows * top, limit, skew, True), portions_of(count, rows * top, limit, skew, False)
    places = jnp.arange(count)

    def named(tallies, offset_by):
        used = int((tallies > 0).sum())
        fixed = max(1, used // 4)
        passed = fixed + (places - fixed + offset_by * (used - fixed)) % max(1, count - fixed)
        return jnp.zeros((count,), jnp.int32).at[ranking[jnp.where(places < fixed, places, passed)]].set(jnp.asarray(tallies, jnp.int32))

    tallies = jnp.where(number % 4 == 0, named(heavy_load, number // 4), named(usual, number - number // 4 - 1))
    mixed = jax.random.permutation(jax.random.fold_in(own, 3), count)
    donor, sink = mixed[0:count // 2 * 2:2], mixed[1:count // 2 * 2:2]
    room = jnp.minimum(tallies[donor] - 1, limit - tallies[sink]) // 2
    room = jnp.where((donor == ranking[0]) | (sink == ranking[0]) | (tallies[sink] == 0), 0, jnp.maximum(room, 0))
    passed = jax.random.randint(jax.random.fold_in(own, 4), (count // 2,), 0, 1 << 20) % (room + 1)
    tallies = tallies.at[donor].add(-passed).at[sink].add(passed)
    members = jnp.searchsorted(jnp.cumsum(tallies), jnp.arange(rows * top), side="right").astype(jnp.int32)
    grid = members.reshape(top, rows).T
    grid = grid[jax.random.permutation(jax.random.fold_in(own, 1), rows)]
    offset_by = jax.random.randint(jax.random.fold_in(own, 2), (rows, 1), 0, top)
    return jnp.take_along_axis(grid, (jnp.arange(top)[None, :] + offset_by) % top, axis=1)


def portions_of(number_of, total, bound, lean, full):
    loads = [(1 << 20) // math.isqrt(rank ** lean) + 1 for rank in range(1, number_of + 1)]
    largest = bound if full else min(bound, max(-(-total // number_of), total * loads[0] // sum(loads)))
    least = 1 if total - largest >= number_of - 1 else 0
    given, rest = [largest] + [least] * (number_of - 1), total - largest - least * (number_of - 1)
    while rest > 0:
        candidates = [i for i in range(1, number_of) if given[i] < largest] or [i for i in range(1, number_of) if given[i] < bound]
        pool, budget = sum([loads[i] for i in candidates]), rest
        for i in candidates:
            extra = min(bound - given[i], max(1, budget * loads[i] // pool), rest)
            given[i] = given[i] + extra
            rest = rest - extra
    return np.array(given)


def gaussian(key, extent, scale, reach, cuts=(), kind=jnp.bfloat16):
    drawn = scale * jax.random.normal(key, extent, jnp.float32)
    if cuts:
        drawn = drawn * level_of(key, extent, cuts, -0.22, 0.18)
    return jnp.clip(drawn, -reach, reach).astype(kind)


def setup_inputs(seed: int = 0) -> dict:
    keys = jax.random.split(jax.random.key(seed), 11)
    imagery = gaussian(keys[0], (BANDS, DATES, PIXELS), 1.0, 6.0, ((1, 16), (2, 16)))
    owner_keys = jax.random.split(jax.random.fold_in(keys[1], 1), PIXELS // PIX_DEV)
    owner_turns = jax.random.permutation(jax.random.fold_in(keys[1], 3), PIXELS // PIX_DEV)
    owner = jax.vmap(lambda own, number: assign_block(jax.random.fold_in(keys[1], 2), own, number, PIX_DEV, N_TILE, 1, CAP, 2))(owner_keys, owner_turns).reshape((PIXELS, 1))
    parcel_local = touch_ends(skewed_ids(keys[2], (PIXELS,), PARC_DEV, 2), jax.random.fold_in(keys[2], 3), 0, PARC_DEV - 1).astype(jnp.int32)
    lift_weight = gaussian(keys[3], (BANDS, CH), BANDS ** -0.5, 2.0)
    depth_weight = gaussian(keys[4], (LAYERS, KSIZE, CH), KSIZE ** -0.5, 2.5, (), jnp.float32)
    point_weight = gaussian(keys[5], (LAYERS, CH, CH), CH ** -0.5, 0.5)
    bn_mean = jnp.clip(jax.random.uniform(keys[6], (LAYERS, CH), jnp.float32, -0.5, 0.5), -0.5, 0.5)
    bn_var = jnp.clip(jnp.exp(jax.random.uniform(keys[7], (LAYERS, CH), jnp.float32, math.log(0.25), math.log(4.0))), 0.25, 4.0)
    bn_gain = jnp.clip(jnp.exp(jax.random.uniform(keys[8], (LAYERS, CH), jnp.float32, math.log(0.5), math.log(2.0))), 0.5, 2.0)
    bn_shift = jnp.clip(jax.random.uniform(keys[9], (LAYERS, CH), jnp.float32, -1.0, 1.0), -1.0, 1.0)
    return {"imagery": imagery, "owner": owner, "parcel_local": parcel_local, "lift_weight": lift_weight, "depth_weight": depth_weight, "point_weight": point_weight, "bn_mean": bn_mean, "bn_var": bn_var, "bn_gain": bn_gain, "bn_shift": bn_shift}


epsilon = 1e-05

def layer_stack(series, lift_weight, depth_weight, point_weight, bn_mean, bn_var, bn_gain, bn_shift):
    hidden = jnp.einsum('bts,bc->tsc', series.astype(jnp.float32), lift_weight.astype(jnp.float32)).astype(jnp.bfloat16)
    for layer in range(depth_weight.shape[0]):
        length = hidden.shape[0]
        half = depth_weight.shape[1] // 2
        widened = jnp.pad(hidden.astype(jnp.float32), ((half, half), (0, 0), (0, 0)))
        spread = jnp.zeros(hidden.shape, jnp.float32)
        for tap in range(depth_weight.shape[1]):
            spread = spread + depth_weight[layer, tap] * widened[tap:tap + length]
        spread = spread.astype(jnp.bfloat16)
        mixed = jnp.einsum('tsc,cd->tsd', spread.astype(jnp.float32), point_weight[layer].astype(jnp.float32))
        factor = bn_gain[layer] / jnp.sqrt(bn_var[layer] + epsilon)
        normed = jax.nn.relu((mixed - bn_mean[layer]) * factor + bn_shift[layer])
        hidden = (0.5 * (normed[0::2] + normed[1::2])).astype(jnp.bfloat16)
    return hidden

def reference(imagery, owner, parcel_local, lift_weight, depth_weight, point_weight, bn_mean, bn_var, bn_gain, bn_shift):
    parcel = owner[:, 0].astype(jnp.int32) * PARC_DEV + parcel_local.astype(jnp.int32)

    def block_sums(total, index):
        start = (index * PIX_DEV).astype(jnp.int32)
        pixels = lax.dynamic_slice_in_dim(imagery, start, PIX_DEV, 2)
        labels = lax.dynamic_slice_in_dim(parcel, start, PIX_DEV, 0)
        features = layer_stack(pixels, lift_weight, depth_weight, point_weight, bn_mean, bn_var, bn_gain, bn_shift)
        partial_value = jax.ops.segment_sum(jnp.transpose(features.astype(jnp.float32), (1, 0, 2)), labels, num_segments=PARCELS)
        return (total + partial_value, None)
    total, unused = lax.scan(block_sums, jnp.zeros((PARCELS, DOUT, CH), jnp.float32), jnp.arange(N_TILE, dtype=jnp.int32))
    counts = jax.ops.segment_sum(jnp.ones((PIXELS,), jnp.int32), parcel, num_segments=PARCELS)
    means = total / jnp.maximum(counts, 1).astype(jnp.float32)[:, None, None]
    return jnp.transpose(means, (1, 0, 2))
```

```python
import jax
import jax.numpy as jnp
import numpy as np
from jax import lax
from jax.experimental import pallas as pl
from jax.experimental.pallas import tpu as pltpu
from jax.sharding import PartitionSpec as P

PARC_DEV = 16
EPSILON = 1e-05
SECTION = 48
BLOCK = 1024

SECTIONS = ((-6, 2), (-4, 4), (0, 4), (4, 4), (8, 2))
FIRST = (0, 1, 1, 2, 2, 3)


def column_table(bands, taps):
    table = np.full((12, 4 * SECTION), -1, np.int32)
    for v in range(6):
        for e in range(2):
            out_date = 2 * (v - 2) + e
            for h in range(2):
                base = h * 16 * taps
                for s in range(2):
                    first, held = SECTIONS[FIRST[v] + s]
                    start = h * 2 * SECTION + s * SECTION
                    for b in range(bands):
                        for t in range(held):
                            k = first + t - out_date + taps // 2
                            if 0 <= k < taps:
                                table[2 * v + e, start + b * held + t] = base + k * 16 + b
                ones = 1 if v == 0 else 0
                table[2 * v + e, h * 2 * SECTION + ones * SECTION + 40] = base + bands
    return table


def prep_kernel(where_ref, table_ref, lift_ref, depth_ref, point_ref, mean_ref, var_ref, gain_ref,
                shift_ref, owner_ref, parcel_ref, w0_ref, w1_ref, b1_ref, counts_ref):
    f32, bf16 = jnp.float32, jnp.bfloat16
    taps = depth_ref.shape[1]
    date_index, tile_index = where_ref[0], where_ref[1]
    factor = gain_ref[...] / jnp.sqrt(var_ref[...] + EPSILON)
    shift = 0.5 * (shift_ref[...] - mean_ref[...] * factor)
    factor = 0.5 * factor
    lift = lift_ref[...]
    rows = jnp.concatenate([lift * depth_ref[0, k : k + 1, :] for k in range(taps)], axis=0)
    base = jnp.dot(rows, point_ref[0].astype(f32), precision=lax.Precision.HIGHEST,
                   preferred_element_type=f32) * factor[0:1]
    place = lax.broadcasted_iota(jnp.int32, base.shape, 0)
    base = jnp.where(place == 10, shift[0:1], base)
    high = base.astype(bf16).astype(f32)
    low = base - high
    spare = jnp.zeros((256 - 2 * base.shape[0], base.shape[1]), f32)
    both = jnp.concatenate([high, low, spare], axis=0).T.astype(bf16)
    width = table_ref.shape[1]
    lane_rows = lax.broadcasted_iota(jnp.int32, (256, width), 0)
    for n in range(12):
        pick = jnp.where(lane_rows == table_ref[n : n + 1, :], 1.0, 0.0).astype(bf16)
        w0_ref[n * 128 : (n + 1) * 128, :] = jnp.dot(
            both, pick, preferred_element_type=f32
        ).astype(bf16)
    mix = (point_ref[1].astype(f32) * factor[1:2]).T
    w1_ref[...] = jnp.zeros(w1_ref.shape, bf16)
    for e in range(2):
        for k in range(taps):
            j = k + e
            pooled_date = 2 * date_index - 2 + j
            inside = jnp.logical_and(pooled_date >= 0, pooled_date < 2 * where_ref[2])
            block = mix * depth_ref[1, k : k + 1, :] * jnp.where(inside, 1.0, 0.0)
            block_high = block.astype(bf16)
            w1_ref[e * 128 : (e + 1) * 128, j * 128 : (j + 1) * 128] = block_high
            w1_ref[e * 128 : (e + 1) * 128, 768 + j * 128 : 768 + (j + 1) * 128] = (
                block - block_high.astype(f32)
            ).astype(bf16)
    b1_ref[...] = jnp.broadcast_to(shift[1:2], b1_ref.shape).T
    mine = jnp.where(owner_ref[...] == tile_index, parcel_ref[...], -1)
    for q in range(PARC_DEV):
        hits = jnp.sum(jnp.where(mine == q, 1.0, 0.0), axis=0, keepdims=True)
        counts_ref[q : q + 1, :] = jnp.broadcast_to(
            jnp.sum(hits, axis=1, keepdims=True), (1, 128)
        )


def main_kernel(m2_ref, m1_ref, own_ref, p1_ref, p2_ref, w0_ref, w1_ref, b1_ref, parcel_ref,
                out_ref, stack_ref):
    f32, bf16 = jnp.float32, jnp.bfloat16
    stack_ref[...] = jnp.zeros(stack_ref.shape, bf16)
    for s in (1, 2, 3):
        row = lax.broadcasted_iota(jnp.int32, (16, BLOCK), 0)
        stack_ref[s * SECTION + 32 : s * SECTION + 48, :] = jnp.where(row == 8, 1.0, 0.0).astype(bf16)
    bias = b1_ref[:, 0:1]

    def pooled_pair(values):
        return (jnp.maximum(values[:128], 0.0) + jnp.maximum(values[128:], 0.0)).astype(bf16)

    def stacked(section):
        part = stack_ref[section * SECTION : (section + 2) * SECTION, :]
        return jnp.concatenate([part, part], axis=0)

    def step(i, total):
        columns = pl.ds(pl.multiple_of(i * BLOCK, BLOCK), BLOCK)
        for s, ref in enumerate((m2_ref, m1_ref, own_ref, p1_ref, p2_ref)):
            held = SECTIONS[s][1]
            for b in range(ref.shape[0]):
                start = s * SECTION + b * held
                stack_ref[start : start + held, :] = ref[b, :, columns]
        pooled = []
        for section, lo, hi in ((0, 0, 1), (1, 1, 3), (2, 3, 5), (3, 5, 6)):
            mixed = jnp.dot(w0_ref[lo * 256 : hi * 256, :], stacked(section),
                            preferred_element_type=f32)
            for v in range(hi - lo):
                pooled.append(pooled_pair(mixed[v * 256 : (v + 1) * 256]))
        series = jnp.concatenate(pooled + pooled, axis=0)
        mixed = jnp.dot(w1_ref[...], series, preferred_element_type=f32)
        features = (
            jnp.maximum(mixed[:128] + bias, 0.0) + jnp.maximum(mixed[128:] + bias, 0.0)
        ).astype(bf16)
        ids = lax.broadcasted_iota(jnp.int32, (out_ref.shape[0], BLOCK), 0)
        member = jnp.where(ids == parcel_ref[:, columns], 1.0, 0.0).astype(bf16)
        return total + lax.dot_general(
            member, features, (((1,), (1,)), ((), ())), preferred_element_type=f32
        )

    out_ref[...] = lax.fori_loop(
        0, own_ref.shape[2] // BLOCK, step, jnp.zeros(out_ref.shape, f32)
    )


def local(imagery, owner, parcel_local, lift_weight, depth_weight, point_weight, bn_mean, bn_var,
          bn_gain, bn_shift):
    tiles = lax.axis_size("tile")
    dates = lax.axis_size("date")
    tile_index = lax.axis_index("tile")
    date_index = lax.axis_index("date")
    bands, date_dev, pix_dev = imagery.shape
    channels = lift_weight.shape[1]
    taps = depth_weight.shape[1]

    def shifted(value, by):
        pairs = [(d, d + by) for d in range(dates) if 0 <= d + by < dates]
        return lax.ppermute(value, "date", pairs)

    before = shifted(imagery, 1)
    after = shifted(imagery, -1)
    before_two = shifted(imagery[:, 2:4], 2)
    after_two = shifted(imagery[:, 0:2], -2)

    owners = owner[:, 0]
    parcel = lax.dynamic_slice_in_dim(owners, tile_index * pix_dev, pix_dev) * PARC_DEV
    parcel = parcel + lax.dynamic_slice_in_dim(parcel_local, tile_index * pix_dev, pix_dev)
    table = jnp.asarray(column_table(bands, taps))
    lift = jnp.pad(lift_weight.astype(jnp.float32), ((0, 16 - bands), (0, 0)))
    where = jnp.stack([date_index, tile_index, jnp.int32(dates)]).astype(jnp.int32)
    vmem = pl.BlockSpec(memory_space=pltpu.VMEM)
    w0, w1, b1, counts = pl.pallas_call(
        prep_kernel,
        out_shape=(
            jax.ShapeDtypeStruct((12 * channels, 4 * SECTION), jnp.bfloat16),
            jax.ShapeDtypeStruct((2 * channels, 12 * channels), jnp.bfloat16),
            jax.ShapeDtypeStruct((channels, channels), jnp.float32),
            jax.ShapeDtypeStruct((PARC_DEV, channels), jnp.float32),
        ),
        in_specs=[pl.BlockSpec(memory_space=pltpu.SMEM)] + [vmem] * 10,
        out_specs=(vmem,) * 4,
        name="prep",
    )(where, table, lift, depth_weight, point_weight, bn_mean, bn_var, bn_gain, bn_shift,
      owners.reshape(-1, 128), parcel_local.reshape(-1, 128))
    sums = pl.pallas_call(
        main_kernel,
        out_shape=jax.ShapeDtypeStruct((tiles * PARC_DEV, channels), jnp.float32),
        in_specs=[vmem] * 9,
        out_specs=vmem,
        scratch_shapes=[pltpu.VMEM((5 * SECTION, BLOCK), jnp.bfloat16)],
        name="encode",
    )(before_two, before, imagery, after, after_two, w0, w1, b1, parcel[None, :])
    arrived = lax.all_to_all(sums, "tile", split_axis=0, concat_axis=0, tiled=True)
    total = jnp.sum(arrived.reshape(tiles, PARC_DEV, channels), axis=0)
    return (total / jnp.maximum(counts, 1.0))[None]


def solution(mesh):
    placed = (P(None, "date", "tile"), P(), P(), P(), P(), P(), P(), P(), P(), P())
    return jax.shard_map(
        local, mesh=mesh, in_specs=placed, out_specs=P("date", "tile", None), check_vma=False
    )
```

```python
import functools

import jax
import jax.numpy as jnp
import numpy as np
from jax import lax
from jax.experimental import pallas as pl
from jax.experimental.pallas import tpu as pltpu
from jax.sharding import PartitionSpec as P

PARC_DEV = 16
EPSILON = 1e-05
SECTION = 48
BLOCK = 1024

SECTIONS = ((-6, 2), (-4, 4), (0, 4), (4, 4), (8, 2))
FIRST = (0, 1, 1, 2, 2, 3)


def column_table(bands, taps):
    table = np.full((12, 4 * SECTION), -1, np.int32)
    for v in range(6):
        for e in range(2):
            out_date = 2 * (v - 2) + e
            for h in range(2):
                base = h * 16 * taps
                for s in range(2):
                    first, held = SECTIONS[FIRST[v] + s]
                    start = h * 2 * SECTION + s * SECTION
                    for b in range(bands):
                        for t in range(held):
                            k = first + t - out_date + taps // 2
                            if 0 <= k < taps:
                                table[2 * v + e, start + b * held + t] = base + k * 16 + b
                ones = 1 if v == 0 else 0
                table[2 * v + e, h * 2 * SECTION + ones * SECTION + 40] = base + bands
    return table


def prep_kernel(date_ref, tile_ref, table_ref, lift_ref, depth_ref, point_ref, mean_ref, var_ref,
                gain_ref, shift_ref, owner_ref, parcel_ref, w0_ref, w1_ref, columns_ref,
                counts_ref, ids_ref, *, dates):
    f32, bf16 = jnp.float32, jnp.bfloat16
    taps = depth_ref.shape[0]
    date_index, tile_index = date_ref[0], tile_ref[0]
    factor = gain_ref[...] / jnp.sqrt(var_ref[...] + EPSILON)
    shift = 0.5 * (shift_ref[...] - mean_ref[...] * factor)
    factor = 0.5 * factor
    lift = lift_ref[...].astype(f32)
    lift = jnp.concatenate([lift, jnp.zeros((16 - lift.shape[0], lift.shape[1]), f32)], axis=0)
    rows = jnp.concatenate([lift * depth_ref[k, 0:1, :] for k in range(taps)], axis=0)
    base = jnp.dot(rows, point_ref[0].astype(f32), precision=lax.Precision.HIGHEST,
                   preferred_element_type=f32) * factor[0:1]
    place = lax.broadcasted_iota(jnp.int32, base.shape, 0)
    base = jnp.where(place == 10, shift[0:1], base)
    high = base.astype(bf16).astype(f32)
    low = base - high
    spare = jnp.zeros((256 - 2 * base.shape[0], base.shape[1]), f32)
    both = jnp.concatenate([high, low, spare], axis=0).T.astype(bf16)
    width = table_ref.shape[1]
    lane_rows = lax.broadcasted_iota(jnp.int32, (256, width), 0)
    for n in range(12):
        pooled_date = 2 * date_index - 2 + n // 2
        inside = jnp.logical_and(pooled_date >= 0, pooled_date < 2 * dates)
        level = jnp.where(inside, 1.0, 0.0)
        pick = jnp.where(lane_rows == table_ref[n : n + 1, :], level, 0.0).astype(bf16)
        w0_ref[n * 128 : (n + 1) * 128, :] = jnp.dot(
            both, pick, preferred_element_type=f32
        ).astype(bf16)
    mix = (point_ref[1].astype(f32) * factor[1:2]).T
    mix_high = mix.astype(bf16)
    w1_ref[:, :128] = mix_high
    w1_ref[:, 128:] = (mix - mix_high.astype(f32)).astype(bf16)
    for k in range(taps):
        columns_ref[k * 128 : (k + 1) * 128, :] = jnp.broadcast_to(
            depth_ref[k, 1:2, :], (128, 128)
        ).T
    columns_ref[taps * 128 : (taps + 1) * 128, :] = jnp.broadcast_to(shift[1:2], (128, 128)).T
    held = ids_ref.shape[0]
    own = pl.ds(pl.multiple_of(tile_index * held, held), held)
    ids_ref[...] = owner_ref[own, :] * PARC_DEV + parcel_ref[own, :]
    mine = jnp.where(owner_ref[...] == tile_index, parcel_ref[...], -1)
    for q in range(PARC_DEV):
        hits = jnp.sum(jnp.where(mine == q, 1.0, 0.0), axis=0, keepdims=True)
        counts_ref[q : q + 1, :] = jnp.broadcast_to(
            jnp.sum(hits, axis=1, keepdims=True), (1, 128)
        )


def main_kernel(m2_ref, m1_ref, own_ref, p1_ref, p2_ref, w0_ref, w1_ref, columns_ref,
                ids_ref, out_ref, stack_ref, *, taps):
    f32, bf16 = jnp.float32, jnp.bfloat16
    stack_ref[...] = jnp.zeros(stack_ref.shape, bf16)
    for s in (1, 2, 3):
        row = lax.broadcasted_iota(jnp.int32, (16, BLOCK), 0)
        stack_ref[s * SECTION + 32 : s * SECTION + 48, :] = jnp.where(row == 8, 1.0, 0.0).astype(bf16)

    def column(k):
        return jnp.concatenate([columns_ref[k * 128 : (k + 1) * 128, :]] * (BLOCK // 128), axis=1)

    def pooled_pair(values):
        return (jnp.maximum(values[:128], 0.0) + jnp.maximum(values[128:], 0.0)).astype(bf16)

    def stacked(section):
        part = stack_ref[section * SECTION : (section + 2) * SECTION, :]
        return jnp.concatenate([part, part], axis=0)

    def step(i, total):
        columns = pl.ds(pl.multiple_of(i * BLOCK, BLOCK), BLOCK)
        for s, ref in enumerate((m2_ref, m1_ref, own_ref, p1_ref, p2_ref)):
            held = SECTIONS[s][1]
            for b in range(ref.shape[0]):
                start = s * SECTION + b * held
                stack_ref[start : start + held, :] = ref[b, :, columns]
        pooled = []
        for section, lo, hi in ((0, 0, 1), (1, 1, 3), (2, 3, 5), (3, 5, 6)):
            mixed = jnp.dot(w0_ref[lo * 256 : hi * 256, :], stacked(section),
                            preferred_element_type=f32)
            for v in range(hi - lo):
                pooled.append(pooled_pair(mixed[v * 256 : (v + 1) * 256]))
        halves = []
        for e in range(2):
            spread = column(0) * pooled[e].astype(f32)
            for k in range(1, taps):
                spread = spread + column(k) * pooled[e + k].astype(f32)
            spread = spread.astype(bf16)
            mixed = jnp.dot(w1_ref[...], jnp.concatenate([spread, spread], axis=0),
                            preferred_element_type=f32)
            halves.append(jnp.maximum(mixed + column(taps), 0.0))
        features = (halves[0] + halves[1]).astype(bf16)
        rows = lax.broadcasted_iota(jnp.int32, (out_ref.shape[0], 128), 0)
        held = BLOCK // 128
        member = jnp.concatenate(
            [
                jnp.where(rows == ids_ref[pl.ds(i * held + m, 1), :], 1.0, 0.0).astype(bf16)
                for m in range(held)
            ],
            axis=1,
        )
        return total + lax.dot_general(
            member, features, (((1,), (1,)), ((), ())), preferred_element_type=f32
        )

    out_ref[...] = lax.fori_loop(
        0, own_ref.shape[2] // BLOCK, step, jnp.zeros(out_ref.shape, f32)
    )


def local(imagery, owner, parcel_local, lift_weight, depth_weight, point_weight, bn_mean, bn_var,
          bn_gain, bn_shift):
    tiles = lax.axis_size("tile")
    dates = lax.axis_size("date")
    tile_index = lax.axis_index("tile")
    date_index = lax.axis_index("date")
    bands, date_dev, pix_dev = imagery.shape
    channels = lift_weight.shape[1]
    taps = depth_weight.shape[1]

    def shifted(value, by):
        pairs = [(d, d + by) for d in range(dates) if 0 <= d + by < dates]
        return lax.ppermute(value, "date", pairs)

    before = shifted(imagery, 1)
    after = shifted(imagery, -1)
    before_two = shifted(imagery[:, 2:4], 2)
    after_two = shifted(imagery[:, 0:2], -2)

    table = jnp.asarray(column_table(bands, taps))
    vmem = pl.BlockSpec(memory_space=pltpu.VMEM)
    smem = pl.BlockSpec(memory_space=pltpu.SMEM)
    w0, w1, columns, counts, ids = pl.pallas_call(
        functools.partial(prep_kernel, dates=dates),
        out_shape=(
            jax.ShapeDtypeStruct((12 * channels, 4 * SECTION), jnp.bfloat16),
            jax.ShapeDtypeStruct((channels, 2 * channels), jnp.bfloat16),
            jax.ShapeDtypeStruct(((taps + 1) * channels, channels), jnp.float32),
            jax.ShapeDtypeStruct((PARC_DEV, channels), jnp.float32),
            jax.ShapeDtypeStruct((pix_dev // 128, 128), jnp.int32),
        ),
        in_specs=[smem] * 2 + [vmem] * 10,
        out_specs=(vmem,) * 5,
        name="prep",
    )(date_index.reshape(1), tile_index.reshape(1), table, lift_weight,
      depth_weight.transpose(1, 0, 2), point_weight, bn_mean, bn_var, bn_gain, bn_shift,
      owner.reshape(-1, 128), parcel_local.reshape(-1, 128))
    sums = pl.pallas_call(
        functools.partial(main_kernel, taps=taps),
        out_shape=jax.ShapeDtypeStruct((tiles * PARC_DEV, channels), jnp.float32),
        in_specs=[vmem] * 9,
        out_specs=vmem,
        scratch_shapes=[pltpu.VMEM((5 * SECTION, BLOCK), jnp.bfloat16)],
        name="encode",
    )(before_two, before, imagery, after, after_two, w0, w1, columns, ids)
    arrived = lax.all_to_all(sums, "tile", split_axis=0, concat_axis=0, tiled=True)
    total = jnp.sum(arrived.reshape(tiles, PARC_DEV, channels), axis=0)
    return (total / jnp.maximum(counts, 1.0))[None]


def solution(mesh):
    placed = (P(None, "date", "tile"), P(), P(), P(), P(), P(), P(), P(), P(), P())
    return jax.shard_map(
        local, mesh=mesh, in_specs=placed, out_specs=P("date", "tile", None), check_vma=False
    )
```

```python
import functools

import jax
import jax.numpy as jnp
import numpy as np
from jax import lax
from jax.experimental import pallas as pl
from jax.experimental.pallas import tpu as pltpu
from jax.sharding import PartitionSpec as P

PARC_DEV = 16
EPSILON = 1e-05
SECTION = 48
BLOCK = 1024
VMEM_LIMIT = 32 * 2**20
UNROLL = 4

SECTIONS = ((-6, 2), (-4, 4), (0, 4), (4, 4), (8, 2))
FIRST = (0, 1, 1, 2, 2, 3)


def column_table(bands, taps):
    table = np.full((12, 4 * SECTION), -1, np.int32)
    for v in range(6):
        for e in range(2):
            out_date = 2 * (v - 2) + e
            for h in range(2):
                base = h * 16 * taps
                for s in range(2):
                    first, held = SECTIONS[FIRST[v] + s]
                    start = h * 2 * SECTION + s * SECTION
                    for b in range(bands):
                        for t in range(held):
                            k = first + t - out_date + taps // 2
                            if 0 <= k < taps:
                                table[2 * v + e, start + b * held + t] = base + k * 16 + b
                ones = 1 if v == 0 else 0
                table[2 * v + e, h * 2 * SECTION + ones * SECTION + 40] = base + bands
    return table


def prep_kernel(date_ref, tile_ref, table_ref, lift_ref, depth_ref, point_ref, mean_ref, var_ref,
                gain_ref, shift_ref, owner_ref, parcel_ref, w0_ref, w1_ref, columns_ref,
                counts_ref, ids_ref, *, dates):
    f32, bf16 = jnp.float32, jnp.bfloat16
    taps = depth_ref.shape[0]
    date_index, tile_index = date_ref[0], tile_ref[0]
    factor = gain_ref[...] / jnp.sqrt(var_ref[...] + EPSILON)
    shift = 0.5 * (shift_ref[...] - mean_ref[...] * factor)
    factor = 0.5 * factor
    lift = lift_ref[...].astype(f32)
    lift = jnp.concatenate([lift, jnp.zeros((16 - lift.shape[0], lift.shape[1]), f32)], axis=0)
    rows = jnp.concatenate([lift * depth_ref[k, 0:1, :] for k in range(taps)], axis=0)
    base = jnp.dot(rows, point_ref[0].astype(f32), precision=lax.Precision.HIGHEST,
                   preferred_element_type=f32) * factor[0:1]
    place = lax.broadcasted_iota(jnp.int32, base.shape, 0)
    base = jnp.where(place == 10, shift[0:1], base)
    high = base.astype(bf16).astype(f32)
    low = base - high
    spare = jnp.zeros((256 - 2 * base.shape[0], base.shape[1]), f32)
    both = jnp.concatenate([high, low, spare], axis=0).T.astype(bf16)
    width = table_ref.shape[1]
    lane_rows = lax.broadcasted_iota(jnp.int32, (256, width), 0)
    for n in range(12):
        pooled_date = 2 * date_index - 2 + n // 2
        inside = jnp.logical_and(pooled_date >= 0, pooled_date < 2 * dates)
        level = jnp.where(inside, 1.0, 0.0)
        pick = jnp.where(lane_rows == table_ref[n : n + 1, :], level, 0.0).astype(bf16)
        w0_ref[n * 128 : (n + 1) * 128, :] = jnp.dot(
            both, pick, preferred_element_type=f32
        ).astype(bf16)
    mix = (point_ref[1].astype(f32) * factor[1:2]).T
    mix_high = mix.astype(bf16)
    w1_ref[:, :128] = mix_high
    w1_ref[:, 128:] = (mix - mix_high.astype(f32)).astype(bf16)
    for k in range(taps):
        columns_ref[k * 128 : (k + 1) * 128, :] = jnp.broadcast_to(
            depth_ref[k, 1:2, :], (128, 128)
        ).T
    columns_ref[taps * 128 : (taps + 1) * 128, :] = jnp.broadcast_to(shift[1:2], (128, 128)).T
    held = ids_ref.shape[0]
    own = pl.ds(pl.multiple_of(tile_index * held, held), held)
    ids_ref[...] = owner_ref[own, :] * PARC_DEV + parcel_ref[own, :]
    mine = jnp.where(owner_ref[...] == tile_index, parcel_ref[...], -1)
    for q in range(PARC_DEV):
        hits = jnp.sum(jnp.where(mine == q, 1.0, 0.0), axis=0, keepdims=True)
        counts_ref[q : q + 1, :] = jnp.broadcast_to(
            jnp.sum(hits, axis=1, keepdims=True), (1, 128)
        )


def fill_stack(stack_ref, sections, refs, columns):
    for place, (s, ref) in enumerate(zip(sections, refs)):
        held = SECTIONS[s][1]
        for b in range(ref.shape[0]):
            start = place * SECTION + b * held
            stack_ref[start : start + held, :] = ref[b, :, columns]


def clear_stack(stack_ref, sections):
    stack_ref[...] = jnp.zeros(stack_ref.shape, jnp.bfloat16)
    row = lax.broadcasted_iota(jnp.int32, (16, BLOCK), 0)
    ones = jnp.where(row == 8, 1.0, 0.0).astype(jnp.bfloat16)
    for place, s in enumerate(sections):
        if SECTIONS[s][1] == 4:
            stack_ref[place * SECTION + 32 : (place + 1) * SECTION, :] = ones


def first_layer(stack_ref, place, w0_ref, lo, hi):
    part = stack_ref[place * SECTION : (place + 2) * SECTION, :]
    mixed = jnp.dot(w0_ref[lo * 256 : hi * 256, :], jnp.concatenate([part, part], axis=0),
                    preferred_element_type=jnp.float32)
    mixed = jnp.maximum(mixed, 0.0)
    return [
        (mixed[v * 256 : v * 256 + 128] + mixed[v * 256 + 128 : (v + 1) * 256]).astype(jnp.bfloat16)
        for v in range(hi - lo)
    ]


def blocks(pixels, step):
    def run(i, carry):
        step(i, pl.ds(pl.multiple_of(i * BLOCK, BLOCK), BLOCK))
        return carry

    lax.fori_loop(0, pixels // BLOCK, run, 0, unroll=UNROLL)


def middle_kernel(m1_ref, own_ref, p1_ref, w0_ref, out_ref, stack_ref):
    sections = (1, 2, 3)
    clear_stack(stack_ref, sections)

    def step(i, columns):
        fill_stack(stack_ref, sections, (m1_ref, own_ref, p1_ref), columns)
        pooled = first_layer(stack_ref, 0, w0_ref, 1, 3) + first_layer(stack_ref, 1, w0_ref, 3, 5)
        for v in range(4):
            out_ref[v * 128 : (v + 1) * 128, columns] = pooled[v]

    blocks(own_ref.shape[2], step)


def main_kernel(m2_ref, m1_ref, p1_ref, p2_ref, w0_ref, w1_ref, columns_ref, ids_ref, middle_ref,
                out_ref, stack_ref, *, taps):
    f32, bf16 = jnp.float32, jnp.bfloat16
    sections = (0, 1, 3, 4)
    clear_stack(stack_ref, sections)
    out_ref[...] = jnp.zeros(out_ref.shape, f32)

    def column(k):
        return jnp.concatenate([columns_ref[k * 128 : (k + 1) * 128, :]] * (BLOCK // 128), axis=1)

    def step(i, columns):
        fill_stack(stack_ref, sections, (m2_ref, m1_ref, p1_ref, p2_ref), columns)
        pooled = (
            first_layer(stack_ref, 0, w0_ref, 0, 1)
            + [middle_ref[v * 128 : (v + 1) * 128, columns] for v in range(4)]
            + first_layer(stack_ref, 2, w0_ref, 5, 6)
        )
        halves = []
        for e in range(2):
            spread = column(0) * pooled[e].astype(f32)
            for k in range(1, taps):
                spread = spread + column(k) * pooled[e + k].astype(f32)
            spread = spread.astype(bf16)
            mixed = jnp.dot(w1_ref[...], jnp.concatenate([spread, spread], axis=0),
                            preferred_element_type=f32)
            halves.append(jnp.maximum(mixed + column(taps), 0.0))
        features = (halves[0] + halves[1]).astype(bf16)
        rows = lax.broadcasted_iota(jnp.int32, (out_ref.shape[0], 128), 0)
        held = BLOCK // 128
        member = jnp.concatenate(
            [
                jnp.where(rows == ids_ref[pl.ds(i * held + m, 1), :], 1.0, 0.0).astype(bf16)
                for m in range(held)
            ],
            axis=1,
        )
        out_ref[...] += lax.dot_general(
            member, features, (((1,), (1,)), ((), ())), preferred_element_type=f32
        )

    blocks(m1_ref.shape[2], step)


def local(imagery, owner, parcel_local, lift_weight, depth_weight, point_weight, bn_mean, bn_var,
          bn_gain, bn_shift):
    tiles = lax.axis_size("tile")
    dates = lax.axis_size("date")
    tile_index = lax.axis_index("tile")
    date_index = lax.axis_index("date")
    bands, date_dev, pix_dev = imagery.shape
    channels = lift_weight.shape[1]
    taps = depth_weight.shape[1]

    def shifted(value, by):
        pairs = [(d, d + by) for d in range(dates) if 0 <= d + by < dates]
        return lax.ppermute(value, "date", pairs)

    before = shifted(imagery, 1)
    after = shifted(imagery, -1)
    before_two = shifted(imagery[:, 2:4], 2)
    after_two = shifted(imagery[:, 0:2], -2)

    def far(*arrays):
        return [pltpu.with_memory_space_constraint(x, pltpu.HBM) for x in arrays]

    table = jnp.asarray(column_table(bands, taps))
    vmem = pl.BlockSpec(memory_space=pltpu.VMEM)
    smem = pl.BlockSpec(memory_space=pltpu.SMEM)
    w0, w1, columns, counts, ids = pl.pallas_call(
        functools.partial(prep_kernel, dates=dates),
        out_shape=(
            pltpu.VMEM((12 * channels, 4 * SECTION), jnp.bfloat16),
            pltpu.VMEM((channels, 2 * channels), jnp.bfloat16),
            pltpu.VMEM(((taps + 1) * channels, channels), jnp.float32),
            pltpu.VMEM((PARC_DEV, channels), jnp.float32),
            pltpu.VMEM((pix_dev // 128, 128), jnp.int32),
        ),
        in_specs=[smem] * 2 + [vmem] * 10,
        out_specs=(vmem,) * 5,
        compiler_params=pltpu.CompilerParams(vmem_limit_bytes=VMEM_LIMIT),
        name="prep",
    )(date_index.reshape(1), tile_index.reshape(1), *far(
        table, lift_weight, depth_weight.transpose(1, 0, 2), point_weight, bn_mean, bn_var,
        bn_gain, bn_shift, owner.reshape(-1, 128), parcel_local.reshape(-1, 128)))

    def near(*arrays):
        return [pltpu.with_memory_space_constraint(x, pltpu.VMEM) for x in arrays]

    middle = pl.pallas_call(
        middle_kernel,
        out_shape=pltpu.VMEM((4 * channels, pix_dev), jnp.bfloat16),
        in_specs=[vmem] * 4,
        out_specs=vmem,
        scratch_shapes=[pltpu.VMEM((3 * SECTION, BLOCK), jnp.bfloat16)],
        compiler_params=pltpu.CompilerParams(vmem_limit_bytes=VMEM_LIMIT),
        name="middle",
    )(*near(before, imagery, after, w0))
    sums = pl.pallas_call(
        functools.partial(main_kernel, taps=taps),
        out_shape=jax.ShapeDtypeStruct((tiles * PARC_DEV, channels), jnp.float32),
        in_specs=[vmem] * 9,
        out_specs=vmem,
        scratch_shapes=[pltpu.VMEM((4 * SECTION, BLOCK), jnp.bfloat16)],
        compiler_params=pltpu.CompilerParams(vmem_limit_bytes=VMEM_LIMIT),
        name="encode",
    )(*near(before_two, before, after, after_two, w0, w1, columns, ids, middle))
    arrived = lax.all_to_all(sums, "tile", split_axis=0, concat_axis=0, tiled=True)
    total = jnp.sum(arrived.reshape(tiles, PARC_DEV, channels), axis=0)
    return (total / jnp.maximum(counts, 1.0))[None]


def solution(mesh):
    placed = (P(None, "date", "tile"), P(), P(), P(), P(), P(), P(), P(), P(), P())
    return jax.shard_map(
        local, mesh=mesh, in_specs=placed, out_specs=P("date", "tile", None), check_vma=False
    )
```

```python
import functools

import jax
import jax.numpy as jnp
import numpy as np
from jax import lax
from jax.experimental import pallas as pl
from jax.experimental.pallas import tpu as pltpu
from jax.sharding import PartitionSpec as P

PARC_DEV = 16
EPSILON = 1e-05
SECTION = 48
BLOCK = 1024
VMEM_LIMIT = 32 * 2**20
UNROLL = 4

SECTIONS = ((-6, 2), (-4, 4), (0, 4), (4, 4), (8, 2))
FIRST = (0, 1, 1, 2, 2, 3)


def column_table(bands, taps):
    table = np.full((12, 4 * SECTION), -1, np.int32)
    for v in range(6):
        for e in range(2):
            out_date = 2 * (v - 2) + e
            for h in range(2):
                base = h * 16 * taps
                for s in range(2):
                    first, held = SECTIONS[FIRST[v] + s]
                    start = h * 2 * SECTION + s * SECTION
                    for b in range(bands):
                        for t in range(held):
                            k = first + t - out_date + taps // 2
                            if 0 <= k < taps:
                                table[2 * v + e, start + b * held + t] = base + k * 16 + b
                ones = 1 if v == 0 else 0
                table[2 * v + e, h * 2 * SECTION + ones * SECTION + 40] = base + bands
    return table


def prep_kernel(date_ref, tile_ref, table_ref, lift_ref, depth_ref, point_ref, mean_ref, var_ref,
                gain_ref, shift_ref, owner_ref, parcel_ref, w0_ref, w1_ref, columns_ref,
                counts_ref, ids_ref, *, dates):
    f32, bf16 = jnp.float32, jnp.bfloat16
    taps = depth_ref.shape[0]
    date_index, tile_index = date_ref[0], tile_ref[0]
    factor = gain_ref[...] / jnp.sqrt(var_ref[...] + EPSILON)
    shift = 0.5 * (shift_ref[...] - mean_ref[...] * factor)
    factor = 0.5 * factor
    lift = lift_ref[...].astype(f32)
    lift = jnp.concatenate([lift, jnp.zeros((16 - lift.shape[0], lift.shape[1]), f32)], axis=0)
    rows = jnp.concatenate([lift * depth_ref[k, 0:1, :] for k in range(taps)], axis=0)
    base = jnp.dot(rows, point_ref[0].astype(f32), precision=lax.Precision.HIGHEST,
                   preferred_element_type=f32) * factor[0:1]
    place = lax.broadcasted_iota(jnp.int32, base.shape, 0)
    base = jnp.where(place == 10, shift[0:1], base)
    high = base.astype(bf16).astype(f32)
    low = base - high
    spare = jnp.zeros((256 - 2 * base.shape[0], base.shape[1]), f32)
    both = jnp.concatenate([high, low, spare], axis=0).T.astype(bf16)
    width = table_ref.shape[1]
    lane_rows = lax.broadcasted_iota(jnp.int32, (256, width), 0)
    for n in range(12):
        pooled_date = 2 * date_index - 2 + n // 2
        inside = jnp.logical_and(pooled_date >= 0, pooled_date < 2 * dates)
        level = jnp.where(inside, 1.0, 0.0)
        pick = jnp.where(lane_rows == table_ref[n : n + 1, :], level, 0.0).astype(bf16)
        w0_ref[n * 128 : (n + 1) * 128, :] = jnp.dot(
            both, pick, preferred_element_type=f32
        ).astype(bf16)
    mix = (point_ref[1].astype(f32) * factor[1:2]).T
    mix_high = mix.astype(bf16)
    w1_ref[:, :128] = mix_high
    w1_ref[:, 128:] = (mix - mix_high.astype(f32)).astype(bf16)
    for k in range(taps):
        columns_ref[k * 128 : (k + 1) * 128, :] = jnp.broadcast_to(
            depth_ref[k, 1:2, :], (128, 128)
        ).T
    columns_ref[taps * 128 : (taps + 1) * 128, :] = jnp.broadcast_to(shift[1:2], (128, 128)).T
    held = ids_ref.shape[0]
    own = pl.ds(pl.multiple_of(tile_index * held, held), held)
    ids_ref[...] = owner_ref[own, :] * PARC_DEV + parcel_ref[own, :]
    mine = jnp.where(owner_ref[...] == tile_index, parcel_ref[...], -1)
    for q in range(PARC_DEV):
        hits = jnp.sum(jnp.where(mine == q, 1.0, 0.0), axis=0, keepdims=True)
        counts_ref[q : q + 1, :] = jnp.broadcast_to(
            jnp.sum(hits, axis=1, keepdims=True), (1, 128)
        )


def fill_stack(stack_ref, sections, refs, columns):
    for place, (s, ref) in enumerate(zip(sections, refs)):
        held = SECTIONS[s][1]
        for b in range(ref[1].shape[0]):
            start = place * SECTION + b * held
            stack_ref[start : start + held, :] = (
                ref[1][b, :, columns]
                if ref[0] is None
                else jnp.where(ref[0], ref[1][b, :, columns], ref[2][b, :, columns])
            )


def clear_stack(stack_ref, sections):
    stack_ref[...] = jnp.zeros(stack_ref.shape, jnp.bfloat16)
    row = lax.broadcasted_iota(jnp.int32, (16, BLOCK), 0)
    ones = jnp.where(row == 8, 1.0, 0.0).astype(jnp.bfloat16)
    for place, s in enumerate(sections):
        if SECTIONS[s][1] == 4:
            stack_ref[place * SECTION + 32 : (place + 1) * SECTION, :] = ones


def first_layer(stack_ref, place, w0_ref, lo, hi):
    part = stack_ref[place * SECTION : (place + 2) * SECTION, :]
    mixed = jnp.dot(w0_ref[lo * 256 : hi * 256, :], jnp.concatenate([part, part], axis=0),
                    preferred_element_type=jnp.float32)
    mixed = jnp.maximum(mixed, 0.0)
    return [
        (mixed[v * 256 : v * 256 + 128] + mixed[v * 256 + 128 : (v + 1) * 256]).astype(jnp.bfloat16)
        for v in range(hi - lo)
    ]


def blocks(pixels, step):
    def run(i, carry):
        step(i, pl.ds(pl.multiple_of(i * BLOCK, BLOCK), BLOCK))
        return carry

    lax.fori_loop(0, pixels // BLOCK, run, 0, unroll=UNROLL)


def middle_kernel(date_ref, partner_ref, own_ref, across_ref, w0_ref, out_ref, stack_ref):
    sections = (1, 2, 3)
    core_odd = date_ref[0] % 2 == 1
    held = (
        (core_odd, partner_ref, across_ref), (None, own_ref), (core_odd, across_ref, partner_ref)
    )
    clear_stack(stack_ref, sections)

    def step(i, columns):
        fill_stack(stack_ref, sections, held, columns)
        pooled = first_layer(stack_ref, 0, w0_ref, 1, 3) + first_layer(stack_ref, 1, w0_ref, 3, 5)
        for v in range(4):
            out_ref[v * 128 : (v + 1) * 128, columns] = pooled[v]

    blocks(own_ref.shape[2], step)


def main_kernel(date_ref, even_ref, odd_ref, partner_ref, across_ref, w0_ref, w1_ref, columns_ref,
                ids_ref, middle_ref, out_ref, stack_ref, *, taps):
    f32, bf16 = jnp.float32, jnp.bfloat16
    sections = (0, 1, 3, 4)
    core_odd = date_ref[0] % 2 == 1
    chip_odd = date_ref[0] // 2 % 2 == 1
    refs = (
        (chip_odd, even_ref, odd_ref), (core_odd, partner_ref, across_ref),
        (core_odd, across_ref, partner_ref), (chip_odd, odd_ref, even_ref),
    )
    clear_stack(stack_ref, sections)
    out_ref[...] = jnp.zeros(out_ref.shape, f32)

    def column(k):
        return jnp.concatenate([columns_ref[k * 128 : (k + 1) * 128, :]] * (BLOCK // 128), axis=1)

    def step(i, columns):
        fill_stack(stack_ref, sections, refs, columns)
        pooled = (
            first_layer(stack_ref, 0, w0_ref, 0, 1)
            + [middle_ref[v * 128 : (v + 1) * 128, columns] for v in range(4)]
            + first_layer(stack_ref, 2, w0_ref, 5, 6)
        )
        halves = []
        for e in range(2):
            spread = column(0) * pooled[e].astype(f32)
            for k in range(1, taps):
                spread = spread + column(k) * pooled[e + k].astype(f32)
            spread = spread.astype(bf16)
            mixed = jnp.dot(w1_ref[...], jnp.concatenate([spread, spread], axis=0),
                            preferred_element_type=f32)
            halves.append(jnp.maximum(mixed + column(taps), 0.0))
        features = (halves[0] + halves[1]).astype(bf16)
        rows = lax.broadcasted_iota(jnp.int32, (out_ref.shape[0], 128), 0)
        held = BLOCK // 128
        member = jnp.concatenate(
            [
                jnp.where(rows == ids_ref[pl.ds(i * held + m, 1), :], 1.0, 0.0).astype(bf16)
                for m in range(held)
            ],
            axis=1,
        )
        out_ref[...] += lax.dot_general(
            member, features, (((1,), (1,)), ((), ())), preferred_element_type=f32
        )

    blocks(across_ref.shape[2], step)


def local(imagery, owner, parcel_local, lift_weight, depth_weight, point_weight, bn_mean, bn_var,
          bn_gain, bn_shift):
    tiles = lax.axis_size("tile")
    dates = lax.axis_size("date")
    tile_index = lax.axis_index("tile")
    date_index = lax.axis_index("date")
    bands, date_dev, pix_dev = imagery.shape
    channels = lift_weight.shape[1]
    taps = depth_weight.shape[1]

    every = range(dates)
    partner = [(d, d ^ 1) for d in every]
    across = [(d, d + 1 if d % 2 else d - 1) for d in every]
    even_pairs = [(d, d - 2 if d // 2 % 2 else d + 2) for d in every]
    odd_pairs = [(d, d + 2 if d // 2 % 2 else d - 2) for d in every]

    def swapped(value, pairs):
        return lax.ppermute(value, "date", [(d, t) for d, t in pairs if 0 <= t < dates])

    by_across = swapped(imagery, across)
    by_partner = swapped(imagery, partner)
    chip_odd = date_index // 2 % 2 == 1
    first, last = imagery[:, 0:2], imagery[:, 2:4]
    by_even = swapped(jnp.where(chip_odd, first, last), even_pairs)
    by_odd = swapped(jnp.where(chip_odd, last, first), odd_pairs)

    def far(*arrays):
        return [pltpu.with_memory_space_constraint(x, pltpu.HBM) for x in arrays]

    table = jnp.asarray(column_table(bands, taps))
    vmem = pl.BlockSpec(memory_space=pltpu.VMEM)
    smem = pl.BlockSpec(memory_space=pltpu.SMEM)
    w0, w1, columns, counts, ids = pl.pallas_call(
        functools.partial(prep_kernel, dates=dates),
        out_shape=(
            pltpu.VMEM((12 * channels, 4 * SECTION), jnp.bfloat16),
            pltpu.VMEM((channels, 2 * channels), jnp.bfloat16),
            pltpu.VMEM(((taps + 1) * channels, channels), jnp.float32),
            pltpu.VMEM((PARC_DEV, channels), jnp.float32),
            pltpu.VMEM((pix_dev // 128, 128), jnp.int32),
        ),
        in_specs=[smem] * 2 + [vmem] * 10,
        out_specs=(vmem,) * 5,
        compiler_params=pltpu.CompilerParams(vmem_limit_bytes=VMEM_LIMIT),
        name="prep",
    )(date_index.reshape(1), tile_index.reshape(1), *far(
        table, lift_weight, depth_weight.transpose(1, 0, 2), point_weight, bn_mean, bn_var,
        bn_gain, bn_shift, owner.reshape(-1, 128), parcel_local.reshape(-1, 128)))

    def near(*arrays):
        return [pltpu.with_memory_space_constraint(x, pltpu.VMEM) for x in arrays]

    middle = pl.pallas_call(
        middle_kernel,
        out_shape=pltpu.VMEM((4 * channels, pix_dev), jnp.bfloat16),
        in_specs=[smem] + [vmem] * 4,
        out_specs=vmem,
        scratch_shapes=[pltpu.VMEM((3 * SECTION, BLOCK), jnp.bfloat16)],
        compiler_params=pltpu.CompilerParams(vmem_limit_bytes=VMEM_LIMIT),
        name="middle",
    )(date_index.reshape(1), *near(by_partner, imagery, by_across, w0))
    sums = pl.pallas_call(
        functools.partial(main_kernel, taps=taps),
        out_shape=jax.ShapeDtypeStruct((tiles * PARC_DEV, channels), jnp.float32),
        in_specs=[smem] + [vmem] * 9,
        out_specs=vmem,
        scratch_shapes=[pltpu.VMEM((4 * SECTION, BLOCK), jnp.bfloat16)],
        compiler_params=pltpu.CompilerParams(vmem_limit_bytes=VMEM_LIMIT),
        name="encode",
    )(date_index.reshape(1),
      *near(by_even, by_odd, by_partner, by_across, w0, w1, columns, ids, middle))
    arrived = lax.all_to_all(sums, "tile", split_axis=0, concat_axis=0, tiled=True)
    total = jnp.sum(arrived.reshape(tiles, PARC_DEV, channels), axis=0)
    return (total / jnp.maximum(counts, 1.0))[None]


def solution(mesh):
    placed = (P(None, "date", "tile"), P(), P(), P(), P(), P(), P(), P(), P(), P())
    return jax.shard_map(
        local, mesh=mesh, in_specs=placed, out_specs=P("date", "tile", None), check_vma=False
    )
```

```python
import functools

import jax
import jax.numpy as jnp
import numpy as np
from jax import lax
from jax.experimental import pallas as pl
from jax.experimental.pallas import tpu as pltpu
from jax.sharding import PartitionSpec as P

PARC_DEV = 16
EPSILON = 1e-05
SECTION = 48
BLOCK = 1024
VMEM_LIMIT = 32 * 2**20
UNROLL = 4

SECTIONS = ((-6, 2), (-4, 4), (0, 4), (4, 4), (8, 2))
FIRST = (0, 1, 1, 2, 2, 3)


def column_table(bands, taps):
    table = np.full((12, 4 * SECTION), -1, np.int32)
    for v in range(6):
        for e in range(2):
            out_date = 2 * (v - 2) + e
            for h in range(2):
                base = h * 16 * taps
                for s in range(2):
                    first, held = SECTIONS[FIRST[v] + s]
                    start = h * 2 * SECTION + s * SECTION
                    for b in range(bands):
                        for t in range(held):
                            k = first + t - out_date + taps // 2
                            if 0 <= k < taps:
                                table[2 * v + e, start + b * held + t] = base + k * 16 + b
                ones = 1 if v == 0 else 0
                table[2 * v + e, h * 2 * SECTION + ones * SECTION + 40] = base + bands
    return table


def prep_kernel(date_ref, tile_ref, table_ref, lift_ref, depth_ref, point_ref, mean_ref, var_ref,
                gain_ref, shift_ref, owner_hbm, parcel_hbm, imagery_hbm, w0_ref, w1_ref,
                columns_ref, counts_ref, ids_ref, own_ref,
                owner_ref, parcel_ref, arrived, *, dates):
    f32, bf16 = jnp.float32, jnp.bfloat16
    copies = [
        pltpu.make_async_copy(source, target, arrived.at[n])
        for n, (source, target) in enumerate(
            ((imagery_hbm, own_ref), (owner_hbm, owner_ref), (parcel_hbm, parcel_ref))
        )
    ]
    for copy in copies:
        copy.start()
    taps = depth_ref.shape[0]
    date_index, tile_index = date_ref[0], tile_ref[0]
    factor = gain_ref[...] / jnp.sqrt(var_ref[...] + EPSILON)
    shift = 0.5 * (shift_ref[...] - mean_ref[...] * factor)
    factor = 0.5 * factor
    lift = lift_ref[...].astype(f32)
    lift = jnp.concatenate([lift, jnp.zeros((16 - lift.shape[0], lift.shape[1]), f32)], axis=0)
    rows = jnp.concatenate([lift * depth_ref[k, 0:1, :] for k in range(taps)], axis=0)
    base = jnp.dot(rows, point_ref[0].astype(f32), precision=lax.Precision.HIGHEST,
                   preferred_element_type=f32) * factor[0:1]
    place = lax.broadcasted_iota(jnp.int32, base.shape, 0)
    base = jnp.where(place == 10, shift[0:1], base)
    high = base.astype(bf16).astype(f32)
    low = base - high
    spare = jnp.zeros((256 - 2 * base.shape[0], base.shape[1]), f32)
    both = jnp.concatenate([high, low, spare], axis=0).T.astype(bf16)
    width = table_ref.shape[1]
    lane_rows = lax.broadcasted_iota(jnp.int32, (256, width), 0)
    for n in range(12):
        pooled_date = 2 * date_index - 2 + n // 2
        inside = jnp.logical_and(pooled_date >= 0, pooled_date < 2 * dates)
        level = jnp.where(inside, 1.0, 0.0)
        pick = jnp.where(lane_rows == table_ref[n : n + 1, :], level, 0.0).astype(bf16)
        w0_ref[n * 128 : (n + 1) * 128, :] = jnp.dot(
            both, pick, preferred_element_type=f32
        ).astype(bf16)
    mix = (point_ref[1].astype(f32) * factor[1:2]).T
    mix_high = mix.astype(bf16)
    w1_ref[:, :128] = mix_high
    w1_ref[:, 128:] = (mix - mix_high.astype(f32)).astype(bf16)
    for k in range(taps):
        columns_ref[k * 128 : (k + 1) * 128, :] = jnp.broadcast_to(
            depth_ref[k, 1:2, :], (128, 128)
        ).T
    columns_ref[taps * 128 : (taps + 1) * 128, :] = jnp.broadcast_to(shift[1:2], (128, 128)).T
    copies[0].wait()
    copies[1].wait()
    copies[2].wait()
    held = ids_ref.shape[0]
    own = pl.ds(pl.multiple_of(tile_index * held, held), held)
    ids_ref[...] = owner_ref[own, :] * PARC_DEV + parcel_ref[own, :]
    mine = jnp.where(owner_ref[...] == tile_index, parcel_ref[...], -1)
    for q in range(PARC_DEV):
        hits = jnp.sum(jnp.where(mine == q, 1.0, 0.0), axis=0, keepdims=True)
        counts_ref[q : q + 1, :] = jnp.broadcast_to(
            jnp.sum(hits, axis=1, keepdims=True), (1, 128)
        )


def fill_stack(stack_ref, sections, refs, columns):
    for place, (s, ref) in enumerate(zip(sections, refs)):
        held = SECTIONS[s][1]
        for b in range(ref[1].shape[0]):
            start = place * SECTION + b * held
            stack_ref[start : start + held, :] = (
                ref[1][b, :, columns]
                if ref[0] is None
                else jnp.where(ref[0], ref[1][b, :, columns], ref[2][b, :, columns])
            )


def clear_stack(stack_ref, sections):
    stack_ref[...] = jnp.zeros(stack_ref.shape, jnp.bfloat16)
    row = lax.broadcasted_iota(jnp.int32, (16, BLOCK), 0)
    ones = jnp.where(row == 8, 1.0, 0.0).astype(jnp.bfloat16)
    for place, s in enumerate(sections):
        if SECTIONS[s][1] == 4:
            stack_ref[place * SECTION + 32 : (place + 1) * SECTION, :] = ones


def first_layer(stack_ref, place, w0_ref, lo, hi):
    part = stack_ref[place * SECTION : (place + 2) * SECTION, :]
    mixed = jnp.dot(w0_ref[lo * 256 : hi * 256, :], jnp.concatenate([part, part], axis=0),
                    preferred_element_type=jnp.float32)
    mixed = jnp.maximum(mixed, 0.0)
    return [
        (mixed[v * 256 : v * 256 + 128] + mixed[v * 256 + 128 : (v + 1) * 256]).astype(jnp.bfloat16)
        for v in range(hi - lo)
    ]


def blocks(pixels, step):
    def run(i, carry):
        step(i, pl.ds(pl.multiple_of(i * BLOCK, BLOCK), BLOCK))
        return carry

    lax.fori_loop(0, pixels // BLOCK, run, 0, unroll=UNROLL)


def middle_kernel(date_ref, partner_ref, own_ref, across_ref, w0_ref, out_ref, stack_ref):
    sections = (1, 2, 3)
    core_odd = date_ref[0] % 2 == 1
    held = (
        (core_odd, partner_ref, across_ref), (None, own_ref), (core_odd, across_ref, partner_ref)
    )
    clear_stack(stack_ref, sections)

    def step(i, columns):
        fill_stack(stack_ref, sections, held, columns)
        pooled = first_layer(stack_ref, 0, w0_ref, 1, 3) + first_layer(stack_ref, 1, w0_ref, 3, 5)
        for v in range(4):
            out_ref[v * 128 : (v + 1) * 128, columns] = pooled[v]

    blocks(own_ref.shape[2], step)


def main_kernel(date_ref, even_ref, odd_ref, partner_ref, across_ref, w0_ref, w1_ref, columns_ref,
                ids_ref, middle_ref, out_ref, stack_ref, *, taps):
    f32, bf16 = jnp.float32, jnp.bfloat16
    sections = (0, 1, 3, 4)
    core_odd = date_ref[0] % 2 == 1
    chip_odd = date_ref[0] // 2 % 2 == 1
    refs = (
        (chip_odd, even_ref, odd_ref), (core_odd, partner_ref, across_ref),
        (core_odd, across_ref, partner_ref), (chip_odd, odd_ref, even_ref),
    )
    clear_stack(stack_ref, sections)
    out_ref[...] = jnp.zeros(out_ref.shape, f32)

    def column(k):
        return jnp.concatenate([columns_ref[k * 128 : (k + 1) * 128, :]] * (BLOCK // 128), axis=1)

    def step(i, columns):
        fill_stack(stack_ref, sections, refs, columns)
        pooled = (
            first_layer(stack_ref, 0, w0_ref, 0, 1)
            + [middle_ref[v * 128 : (v + 1) * 128, columns] for v in range(4)]
            + first_layer(stack_ref, 2, w0_ref, 5, 6)
        )
        halves = []
        for e in range(2):
            spread = column(0) * pooled[e].astype(f32)
            for k in range(1, taps):
                spread = spread + column(k) * pooled[e + k].astype(f32)
            spread = spread.astype(bf16)
            mixed = jnp.dot(w1_ref[...], jnp.concatenate([spread, spread], axis=0),
                            preferred_element_type=f32)
            halves.append(jnp.maximum(mixed + column(taps), 0.0))
        features = (halves[0] + halves[1]).astype(bf16)
        rows = lax.broadcasted_iota(jnp.int32, (out_ref.shape[0], 128), 0)
        held = BLOCK // 128
        member = jnp.concatenate(
            [
                jnp.where(rows == ids_ref[pl.ds(i * held + m, 1), :], 1.0, 0.0).astype(bf16)
                for m in range(held)
            ],
            axis=1,
        )
        out_ref[...] += lax.dot_general(
            member, features, (((1,), (1,)), ((), ())), preferred_element_type=f32
        )

    blocks(across_ref.shape[2], step)


def local(imagery, owner, parcel_local, lift_weight, depth_weight, point_weight, bn_mean, bn_var,
          bn_gain, bn_shift):
    tiles = lax.axis_size("tile")
    dates = lax.axis_size("date")
    tile_index = lax.axis_index("tile")
    date_index = lax.axis_index("date")
    bands, date_dev, pix_dev = imagery.shape
    channels = lift_weight.shape[1]
    taps = depth_weight.shape[1]

    every = range(dates)
    partner = [(d, d ^ 1) for d in every]
    across = [(d, d + 1 if d % 2 else d - 1) for d in every]
    even_pairs = [(d, d - 2 if d // 2 % 2 else d + 2) for d in every]
    odd_pairs = [(d, d + 2 if d // 2 % 2 else d - 2) for d in every]

    def swapped(value, pairs):
        return lax.ppermute(value, "date", [(d, t) for d, t in pairs if 0 <= t < dates])

    by_across = swapped(imagery, across)
    by_partner = swapped(imagery, partner)
    chip_odd = date_index // 2 % 2 == 1
    first, last = imagery[:, 0:2], imagery[:, 2:4]
    by_even = swapped(jnp.where(chip_odd, first, last), even_pairs)
    by_odd = swapped(jnp.where(chip_odd, last, first), odd_pairs)

    def far(*arrays):
        return [pltpu.with_memory_space_constraint(x, pltpu.HBM) for x in arrays]

    table = jnp.asarray(column_table(bands, taps))
    vmem = pl.BlockSpec(memory_space=pltpu.VMEM)
    smem = pl.BlockSpec(memory_space=pltpu.SMEM)
    w0, w1, columns, counts, ids, own = pl.pallas_call(
        functools.partial(prep_kernel, dates=dates),
        out_shape=(
            pltpu.VMEM((12 * channels, 4 * SECTION), jnp.bfloat16),
            pltpu.VMEM((channels, 2 * channels), jnp.bfloat16),
            pltpu.VMEM(((taps + 1) * channels, channels), jnp.float32),
            pltpu.VMEM((PARC_DEV, channels), jnp.float32),
            pltpu.VMEM((pix_dev // 128, 128), jnp.int32),
            pltpu.VMEM(imagery.shape, imagery.dtype),
        ),
        in_specs=[smem] * 2 + [vmem] * 8 + [pl.BlockSpec(memory_space=pltpu.HBM)] * 3,
        out_specs=(vmem,) * 6,
        scratch_shapes=[
            pltpu.VMEM((tiles * pix_dev // 128, 128), jnp.int32),
            pltpu.VMEM((tiles * pix_dev // 128, 128), jnp.int32),
            pltpu.SemaphoreType.DMA((3,)),
        ],
        compiler_params=pltpu.CompilerParams(vmem_limit_bytes=VMEM_LIMIT),
        name="prep",
    )(date_index.reshape(1), tile_index.reshape(1), *far(
        table, lift_weight, depth_weight.transpose(1, 0, 2), point_weight, bn_mean, bn_var,
        bn_gain, bn_shift, owner.reshape(-1, 128), parcel_local.reshape(-1, 128), imagery))

    def near(*arrays):
        return [pltpu.with_memory_space_constraint(x, pltpu.VMEM) for x in arrays]

    middle = pl.pallas_call(
        middle_kernel,
        out_shape=pltpu.VMEM((4 * channels, pix_dev), jnp.bfloat16),
        in_specs=[smem] + [vmem] * 4,
        out_specs=vmem,
        scratch_shapes=[pltpu.VMEM((3 * SECTION, BLOCK), jnp.bfloat16)],
        compiler_params=pltpu.CompilerParams(vmem_limit_bytes=VMEM_LIMIT),
        name="middle",
    )(date_index.reshape(1), *near(by_partner, own, by_across, w0))
    sums = pl.pallas_call(
        functools.partial(main_kernel, taps=taps),
        out_shape=jax.ShapeDtypeStruct((tiles * PARC_DEV, channels), jnp.float32),
        in_specs=[smem] + [vmem] * 9,
        out_specs=vmem,
        scratch_shapes=[pltpu.VMEM((4 * SECTION, BLOCK), jnp.bfloat16)],
        compiler_params=pltpu.CompilerParams(vmem_limit_bytes=VMEM_LIMIT),
        name="encode",
    )(date_index.reshape(1),
      *near(by_even, by_odd, by_partner, by_across, w0, w1, columns, ids, middle))
    arrived = lax.all_to_all(sums, "tile", split_axis=0, concat_axis=0, tiled=True)
    total = jnp.sum(arrived.reshape(tiles, PARC_DEV, channels), axis=0)
    return (total / jnp.maximum(counts, 1.0))[None]


def solution(mesh):
    placed = (P(None, "date", "tile"), P(), P(), P(), P(), P(), P(), P(), P(), P())
    return jax.shard_map(
        local, mesh=mesh, in_specs=placed, out_specs=P("date", "tile", None), check_vma=False
    )
```
